32 devices in a mesh: dp: 4 (over z), seq: 8 (over y, x, core).
Axes of the slice: x: 2, y: 2, z: 4, core: 2. Of those that a mesh axis runs over, the one named last changes fastest.
Arguments:
- hidden: bfloat16 [8, 2048, 1536], P('dp', 'seq'), may hold values from -8 to 8
- lengths: int32 [8], P('dp'), may hold values from 1024 to 2048, as said below
- cotangent: bfloat16 [8, 2048, 1536], P('dp', 'seq'), may hold values from -6 to 6
- norm_gain: bfloat16 [2, 1536], P(None, 'dp'), may hold values from 0.5 to 1.5
- in_weight: bfloat16 [2, 1536, 6448], P(None, 'dp'), may hold values from -0.15625 to 0.15625
- conv_weight: bfloat16 [2, 4, 3328], P(None, None, 'dp'), may hold values from -3 to 3
- conv_bias: bfloat16 [2, 3328], P(None, 'dp'), may hold values from -1.5 to 1.5
- dt_bias: bfloat16 [2, 48], P(None, 'dp'), may hold values from -9 to -3
- decay_log: bfloat16 [2, 48], P(None, 'dp'), may hold values from -1 to 1.5
- skip_gain: bfloat16 [2, 48], P(None, 'dp'), may hold values from 0.5 to 2
- gate_gain: bfloat16 [2, 3072], P(None, 'dp'), may hold values from 0.5 to 1.5
- out_weight: bfloat16 [2, 3072, 1536], P(None, 'dp'), may hold values from -0.109375 to 0.109375
Outputs:
- output: float32 [8, 2048, 1536], P('dp', 'seq')
- grad_hidden: float32 [8, 2048, 1536], P('dp', 'seq')
- grad_norm_gain: float32 [2, 1536], P(None, 'dp')
- grad_in_weight: float32 [2, 1536, 6448], P(None, 'dp')
- grad_conv_weight: float32 [2, 4, 3328], P(None, None, 'dp')
- grad_conv_bias: float32 [2, 3328], P(None, 'dp')
- grad_dt_bias: float32 [2, 48], P(None, 'dp')
- grad_decay_log: float32 [2, 48], P(None, 'dp')
- grad_skip_gain: float32 [2, 48], P(None, 'dp')
- grad_gate_gain: float32 [2, 3072], P(None, 'dp')
- grad_out_weight: float32 [2, 3072, 1536], P(None, 'dp')
- norm_stats: float32 [2, 2], replicated
The draws below stay inside these ranges and needn't reach their ends.
Inputs may be any that keep to these rules, and one draw needn't show every extreme that they name: Sequence s has valid slots 0 .. lengths[s] - 1; in every draw one sequence has all 2048 slots valid and another exactly 1024.
All inputs are finite; a program needn't handle non-finite values.
Results may differ from the reference program's by a relative error of at most 0.02.
Values may be sent and summed in bfloat16 or wider, within the bound.
A program may use at most 576 MiB of HBM per device.

```python
from functools import partial
import jax
import jax.numpy as jnp
from jax import lax

D = 1536
HEADS = 48
HEAD_DIM = 64
STATE = 128
CONV = 4
BLOCK = 256
LAYERS = 2
MIN_LEN = 1024
DIN = 3072
XBC = 3328
PROJ = 6448
SLOTS = 2048
SEQS = 8


def draw_lengths(key, part):
    first_key, second_key, third_key = jax.random.split(key, 3)
    drawn = jax.random.randint(first_key, (SEQS,), MIN_LEN, SLOTS + 1)
    longest = jax.random.randint(second_key, (), 0, SEQS)
    shortest = (longest + 1 + jax.random.randint(third_key, (), 0, SEQS - 1)) % SEQS
    return drawn.at[longest].set(SLOTS).at[shortest].set(MIN_LEN).astype(jnp.int32)


def draw_hidden(key, part):
    value_key = jax.random.fold_in(key, 17)
    place = jnp.arange(SLOTS, dtype=jnp.float32) / SLOTS
    base = jax.random.normal(value_key, (SEQS, SLOTS, D), jnp.float32)
    scale = 0.5 * jnp.exp(jnp.log(4.0) * place)
    return jnp.clip(base * scale[None, :, None], -8.0, 8.0).astype(jnp.bfloat16)


def block_scale(key, extent, pieces, smallest, top_value):
    loudness, own = 1.0, jax.random.fold_in(key, 6)
    for axis_at, shards_of in pieces:
        steps = jnp.exp(jax.random.uniform(jax.random.fold_in(own, axis_at), (shards_of,), jnp.float32, smallest / len(pieces), top_value / len(pieces)))
        loudness = loudness * jnp.repeat(steps, extent[axis_at] // shards_of).reshape([-1 if axis == axis_at else 1 for axis in range(len(extent))])
    return loudness


def bell_draw(stream_key, dims, deviation, reach, cuts=(), held_as=jnp.bfloat16):
    loudness = block_scale(stream_key, dims, cuts, -0.22, 0.18) if cuts else 1.0
    result = jax.random.normal(stream_key, dims, jnp.float32) * deviation * loudness
    return jnp.minimum(jnp.maximum(result, -reach), reach).astype(held_as)


def setup_inputs(seed: int = 0) -> dict:
    keys = jax.random.split(jax.random.key(seed), 13)
    return {
        "hidden": draw_hidden(jax.random.fold_in(keys[12], 71), 0),
        "lengths": draw_lengths(jax.random.fold_in(keys[12], 71), 0),
        "cotangent": bell_draw(keys[2], (SEQS, SLOTS, D), 1.0, 6.0, ((0, 4), (1, 8))),
        "norm_gain": jnp.clip(1.0 + 0.1 * jax.random.normal(keys[3], (LAYERS, D), jnp.float32), 0.5, 1.5).astype(jnp.bfloat16),
        "in_weight": bell_draw(keys[4], (LAYERS, D, PROJ), D ** -0.5, 0.15625, ((1, 4),)),
        "conv_weight": bell_draw(keys[5], (LAYERS, CONV, XBC), CONV ** -0.5, 3.0, ((2, 4),)),
        "conv_bias": bell_draw(keys[6], (LAYERS, XBC), 0.3, 1.5, ((1, 4),)),
        "dt_bias": jnp.clip(-9.0 + 6.0 * jax.random.uniform(keys[7], (LAYERS, HEADS), jnp.float32) ** block_scale(keys[7], (LAYERS, HEADS), ((1, 4),), -0.2, 0.2), -9.0, -3.0).astype(jnp.bfloat16),
        "decay_log": jnp.clip(-1.0 + 2.5 * jax.random.uniform(keys[8], (LAYERS, HEADS), jnp.float32) ** block_scale(keys[8], (LAYERS, HEADS), ((1, 4),), -0.2, 0.2), -1.0, 1.5).astype(jnp.bfloat16),
        "skip_gain": jnp.clip(0.5 + 1.5 * jax.random.uniform(keys[9], (LAYERS, HEADS), jnp.float32) ** block_scale(keys[9], (LAYERS, HEADS), ((1, 4),), -0.2, 0.2), 0.5, 2.0).astype(jnp.bfloat16),
        "gate_gain": jnp.clip(1.0 + 0.1 * jax.random.normal(keys[10], (LAYERS, DIN), jnp.float32), 0.5, 1.5).astype(jnp.bfloat16),
        "out_weight": bell_draw(keys[11], (LAYERS, DIN, D), DIN ** -0.5, 0.109375, ((1, 4),)),
    }


epsilon = 1e-05
highest = lax.Precision.HIGHEST

@jax.custom_vjp
def low(v):
    return lax.optimization_barrier(v.astype(jnp.bfloat16)).astype(jnp.float32)

@jax.custom_vjp
def low_back(v):
    return v

def low_keep(v):
    return (low(v), None)

def low_pass(kept, grad):
    return (grad,)

def back_keep(v):
    return (v, None)

def back_low(kept, grad):
    return (low(grad),)
low.defvjp(low_keep, low_pass)
low_back.defvjp(back_keep, back_low)

def norm_rows(values, scales):
    return values * lax.rsqrt(lax.optimization_barrier(jnp.mean(values * values, -1, keepdims=True)) + epsilon) * scales

def causal(values, kernel, offset):
    length = values.shape[-2]
    widths = [(0, 0)] * (values.ndim - 2) + [(kernel.shape[0] - 1, 0), (0, 0)]
    padded = jnp.pad(values, widths)
    running = jnp.expand_dims(offset, -2)
    for tap_index in range(kernel.shape[0]):
        running = running + jnp.expand_dims(kernel[tap_index], -2) * padded[..., tap_index:tap_index + length, :]
    return running

def prepare(x_raw, bc_raw, step_raw, conv_x, bias_x, conv_bc, bias_bc, step_offset, decay_rate):
    x_active = jax.nn.silu(causal(x_raw, conv_x, bias_x))
    bc_active = jax.nn.silu(causal(bc_raw, conv_bc, bias_bc))
    step_sizes = jax.nn.softplus(step_raw + step_offset[:, None])
    log_decay = -step_sizes * jnp.exp(decay_rate)[:, None]
    cumulative = jnp.cumsum(log_decay.reshape(log_decay.shape[0], -1, BLOCK), -1)
    return (x_active, bc_active, step_sizes, cumulative)

def weigh_block(scores, cumulative, step_sizes):
    block_size = cumulative.shape[-1]
    lower_mask = jnp.arange(block_size)[:, None] >= jnp.arange(block_size)[None, :]
    spread = cumulative[..., :, None] - cumulative[..., None, :]
    decay = jnp.where(lower_mask, jnp.exp(jnp.where(lower_mask, spread, 0.0)), 0.0)
    return scores * decay * step_sizes[..., None, :]

def across(values, write_rows, read_rows, step_sizes, cumulative, skip_scale):
    totals = cumulative[..., -1]
    weights = jnp.exp(totals[..., None] - cumulative) * step_sizes
    weighted = weights[..., None] * values
    states = jnp.einsum('kbjp,bjn->kbpn', weighted, write_rows, precision=highest)
    block_ends = jnp.cumsum(totals, -1)
    starts = block_ends - totals
    block_count = totals.shape[-1]
    before_mask = jnp.arange(block_count)[:, None] > jnp.arange(block_count)[None, :]
    spread = starts[..., :, None] - block_ends[..., None, :]
    carried_decay = jnp.where(before_mask, jnp.exp(jnp.where(before_mask, spread, 0.0)), 0.0)
    entering = jnp.einsum('kcd,kdpn->kcpn', carried_decay, states, precision=highest)
    readout = jnp.einsum('bin,kbpn->kbip', read_rows, entering, precision=highest)
    return jnp.exp(cumulative)[..., None] * readout + skip_scale[:, None, None, None] * values

def gated_norm(values, gate_in, scales):
    gated = values * jax.nn.silu(gate_in)
    return gated * lax.rsqrt(lax.optimization_barrier(jnp.mean(gated * gated, -1, keepdims=True)) + epsilon) * scales

def mixer(hidden_row, weights):
    norm_scale, proj_in, conv_kernel, conv_offset, step_offset, decay_rate, skip_scale, gate_scale, proj_out = weights
    length = hidden_row.shape[0]
    blocks = length // BLOCK
    normed = norm_rows(hidden_row, norm_scale)
    projected = low_back(jnp.dot(low(normed), proj_in, precision=highest))
    gate_in = projected[:, :DIN]
    x_raw = low(low_back(projected[:, DIN:2 * DIN]))
    bc_raw = low(projected[:, 2 * DIN:2 * DIN + 2 * STATE])
    step_raw = low(low_back(projected[:, 2 * DIN + 2 * STATE:]))
    x_heads = x_raw.reshape(length, HEADS, HEAD_DIM).transpose(1, 0, 2)
    x_active, bc_active, step_sizes, cumulative = prepare(x_heads, bc_raw, step_raw.T, conv_kernel[:, :DIN].reshape(CONV, HEADS, HEAD_DIM), conv_offset[:DIN].reshape(HEADS, HEAD_DIM), conv_kernel[:, DIN:], conv_offset[DIN:], step_offset, decay_rate)
    x_low = low(x_active).reshape(HEADS, blocks, BLOCK, HEAD_DIM)
    write_rows = low(bc_active[:, :STATE]).reshape(blocks, BLOCK, STATE)
    read_rows = low(bc_active[:, STATE:]).reshape(blocks, BLOCK, STATE)
    step_blocks = step_sizes.reshape(HEADS, blocks, BLOCK)
    scores = jnp.einsum('bin,bjn->bij', read_rows, write_rows, precision=highest)
    mixing = low(weigh_block(scores, cumulative, step_blocks))
    direct = jnp.einsum('kbij,kbjp->kbip', mixing, x_low, precision=highest)
    heads_out = low(low_back(direct + across(x_low, write_rows, read_rows, step_blocks, cumulative, skip_scale)))
    y_tokens = heads_out.reshape(HEADS, length, HEAD_DIM).transpose(1, 0, 2).reshape(length, DIN)
    gated_out = gated_norm(y_tokens, gate_in, gate_scale)
    return low_back(jnp.dot(low(gated_out), proj_out, precision=highest))

def reference(hidden, lengths, cotangent, norm_gain, in_weight, conv_weight, conv_bias, dt_bias, decay_log, skip_gain, gate_gain, out_weight):
    valid_mask = (jnp.arange(SLOTS)[None, :] < lengths[:, None]).astype(jnp.float32)
    params = tuple((array.astype(jnp.float32) for array in (norm_gain, in_weight, conv_weight, conv_bias, dt_bias, decay_log, skip_gain, gate_gain, out_weight)))

    def forward(start, weights):
        hidden_now = start
        squares = []
        for layer_index in range(LAYERS):
            chosen = tuple((array[layer_index] for array in weights))
            mixer_out = lax.map(jax.checkpoint(partial(mixer, weights=chosen)), hidden_now)
            squares.append(jnp.sum(hidden_now * hidden_now * valid_mask[..., None]))
            squares.append(jnp.sum(mixer_out * mixer_out * valid_mask[..., None]))
            hidden_now = hidden_now + mixer_out
        return (hidden_now * valid_mask[..., None], jnp.stack(squares))
    output, pullback, squares = jax.vjp(forward, hidden.astype(jnp.float32), params, has_aux=True)
    grad_start, grads = pullback(cotangent.astype(jnp.float32))
    norm_stats = jnp.sqrt(squares.reshape(LAYERS, 2) / (jnp.sum(valid_mask) * D))
    return (output, grad_start, grads[0], grads[1], grads[2], grads[3], grads[4], grads[5], grads[6], grads[7], grads[8], norm_stats)
```

```python
import functools

import jax
import jax.numpy as jnp
from jax import lax
from jax.experimental import pallas as pl
from jax.experimental.pallas import tpu as pltpu
from jax.sharding import PartitionSpec as P

D = 1536
HEADS = 48
HEAD_DIM = 64
STATE = 128
CONV = 4
BLOCK = 256
LAYERS = 2
DIN = 3072
XBC = DIN + 2 * STATE
REST = XBC + HEADS
PAIRS = HEADS // 2
LANES = 128
HALO = 8

epsilon = 1e-05
highest = lax.Precision.HIGHEST
f32 = jnp.float32
bf16 = jnp.bfloat16
NEG = -1e30


def dot(a, b, ca, cb):
    return lax.dot_general(a, b, (((ca,), (cb,)), ((), ())), preferred_element_type=f32)


def params(semantics, limit=None):
    return pltpu.CompilerParams(dimension_semantics=semantics, vmem_limit_bytes=limit)


def lane_is_low(rows):
    return lax.broadcasted_iota(jnp.int32, (rows, LANES), 1) < HEAD_DIM


def convolve(ext, raw, halo, par):
    rows = raw.shape[0]
    ext[0:HALO, :] = halo.astype(f32)
    ext[HALO : HALO + rows, :] = raw.astype(f32)
    total = par[CONV : CONV + 1, :]
    for tap in range(CONV):
        total = total + par[tap : tap + 1, :] * ext[pl.ds(HALO - CONV + 1 + tap, rows), :]
    return total


def causal_mask():
    i = lax.broadcasted_iota(jnp.int32, (BLOCK, BLOCK), 0)
    j = lax.broadcasted_iota(jnp.int32, (BLOCK, BLOCK), 1)
    return i >= j


def scan_kernel(raw, halo, bc, bc_halo, par, par_bc, rows_ref, direct, states, wbrc, ext, ext_bc, scores):
    pair = pl.program_id(1)

    @pl.when(pair == 0)
    def _():
        conv = convolve(ext_bc, bc[...], bc_halo[...], par_bc)
        act = (conv * jax.nn.sigmoid(conv)).astype(bf16)
        wbrc[...] = act
        scores[...] = dot(act[:, STATE:], act[:, :STATE], 1, 1)

    conv = convolve(ext, raw[...], halo[...], par)
    x = (conv * jax.nn.sigmoid(conv)).astype(bf16).astype(f32)
    rows = rows_ref[0, 0]
    cols = rows.T
    low = lane_is_low(BLOCK)
    mask = causal_mask()
    total = par[CONV + 1 : CONV + 2, :] * x
    for a in range(2):
        mine = low if a == 0 else jnp.logical_not(low)
        x_a = jnp.where(mine, x, 0.0).astype(bf16)
        spread = cols[:, 2 + a : 3 + a] - rows[2 + a : 3 + a, :]
        decay = jnp.exp(jnp.where(mask, spread, NEG))
        mixing = (scores[...] * decay * rows[a : a + 1, :]).astype(bf16)
        total = total + dot(mixing, x_a, 1, 0)
    direct[...] = total
    weight = jnp.where(low, cols[:, 6:7] * cols[:, 0:1], cols[:, 7:8] * cols[:, 1:2])
    states[0, 0] = dot((weight * x).astype(bf16), wbrc[:, :STATE], 0, 0).astype(bf16)


def scan_forward(proj, par, rows):
    seqs = rows.shape[0]
    halo_at = seqs * BLOCK // HALO
    return pl.pallas_call(
        scan_kernel,
        grid=(seqs, PAIRS),
        in_specs=[
            pl.BlockSpec((BLOCK, LANES), lambda s, p: (s, p)),
            pl.BlockSpec((HALO, LANES), lambda s, p: (halo_at + s, p)),
            pl.BlockSpec((BLOCK, 2 * STATE), lambda s, p: (s, DIN // (2 * STATE))),
            pl.BlockSpec((HALO, 2 * STATE), lambda s, p: (halo_at + s, DIN // (2 * STATE))),
            pl.BlockSpec((8, LANES), lambda s, p: (0, p)),
            pl.BlockSpec((8, 2 * STATE), lambda s, p: (0, DIN // (2 * STATE))),
            pl.BlockSpec((1, 1, 8, BLOCK), lambda s, p: (s, p, 0, 0)),
        ],
        out_specs=[
            pl.BlockSpec((BLOCK, LANES), lambda s, p: (s, p)),
            pl.BlockSpec((1, 1, LANES, STATE), lambda s, p: (s, p, 0, 0)),
            pl.BlockSpec((BLOCK, 2 * STATE), lambda s, p: (s, 0)),
        ],
        out_shape=[
            jax.ShapeDtypeStruct((seqs * BLOCK, DIN), f32),
            jax.ShapeDtypeStruct((seqs, PAIRS, LANES, STATE), bf16),
            jax.ShapeDtypeStruct((seqs * BLOCK, 2 * STATE), bf16),
        ],
        scratch_shapes=[
            pltpu.VMEM((BLOCK + HALO, LANES), f32),
            pltpu.VMEM((BLOCK + HALO, 2 * STATE), f32),
            pltpu.VMEM((BLOCK, BLOCK), f32),
        ],
        compiler_params=params(("arbitrary", "arbitrary")),
        cost_estimate=pl.CostEstimate(
            flops=seqs * PAIRS * 4 * BLOCK * BLOCK * LANES,
            bytes_accessed=seqs * BLOCK * DIN * 6,
            transcendentals=seqs * HEADS * BLOCK * BLOCK,
        ),
        name="scan_forward",
    )(proj, proj, proj, proj, par, par, rows)


def gate_kernel(direct, gate, rc, rows_ref, entering, gain, y_ref, out, kept):
    tile = direct.shape[0]
    low = lane_is_low(tile)

    def body(pair, squares):
        at = pl.ds(pl.multiple_of(pair * LANES, LANES), LANES)
        cols = rows_ref[0, pair].T
        readout = dot(rc[...], entering[0, pair], 1, 1)
        y = (direct[:, at] + jnp.where(low, cols[:, 4:5], cols[:, 5:6]) * readout).astype(bf16)
        y_ref[:, at] = y
        g = gate[:, at].astype(f32)
        gated = y.astype(f32) * (g * jax.nn.sigmoid(g))
        kept[:, at] = gated
        return squares + gated * gated

    squares = lax.fori_loop(0, PAIRS, body, jnp.zeros((tile, LANES), f32))
    scale = lax.rsqrt(jnp.sum(squares, -1, keepdims=True) * (1.0 / DIN) + epsilon)
    out[...] = (kept[...] * scale * gain[...]).astype(bf16)


def gate_forward(direct, gate, wbrc, rows, entering, gain):
    seqs = rows.shape[0]
    tile = 128
    parts = BLOCK // tile
    wide = pl.BlockSpec((tile, DIN), lambda s, r: (s * parts + r, 0))
    return pl.pallas_call(
        gate_kernel,
        grid=(seqs, parts),
        in_specs=[
            wide,
            wide,
            pl.BlockSpec((tile, STATE), lambda s, r: (s * parts + r, 1)),
            pl.BlockSpec((1, PAIRS, 8, tile), lambda s, r: (s, 0, 0, r)),
            pl.BlockSpec((1, PAIRS, LANES, STATE), lambda s, r: (s, 0, 0, 0)),
            pl.BlockSpec((1, DIN), lambda s, r: (0, 0)),
        ],
        out_specs=[wide, wide],
        out_shape=[
            jax.ShapeDtypeStruct((seqs * BLOCK, DIN), bf16),
            jax.ShapeDtypeStruct((seqs * BLOCK, DIN), bf16),
        ],
        scratch_shapes=[pltpu.VMEM((tile, DIN), f32)],
        compiler_params=params(("arbitrary", "arbitrary")),
        cost_estimate=pl.CostEstimate(
            flops=2 * seqs * BLOCK * DIN * STATE,
            bytes_accessed=seqs * BLOCK * DIN * 10,
            transcendentals=seqs * BLOCK * DIN,
        ),
        name="gate_forward",
    )(direct, gate, wbrc, rows, entering, gain)


def gate_back_kernel(grad, y_ref, gate, gain, rc, rows_ref, g_y, g_gate, g_entering, g_gain):
    low = lane_is_low(BLOCK)

    def at_pair(pair):
        return pl.ds(pl.multiple_of(pair * LANES, LANES), LANES)

    def parts(pair):
        at = at_pair(pair)
        g = gate[:, at].astype(f32)
        sig = jax.nn.sigmoid(g)
        y = y_ref[:, at].astype(f32)
        return at, g, sig, y, y * (g * sig)

    def first(pair, sums):
        at, _, _, _, gated = parts(pair)
        return sums[0] + gated * gated, sums[1] + grad[:, at] * gain[:, at] * gated

    zero = jnp.zeros((BLOCK, LANES), f32)
    squares, products = lax.fori_loop(0, PAIRS, first, (zero, zero))
    scale = lax.rsqrt(jnp.sum(squares, -1, keepdims=True) * (1.0 / DIN) + epsilon)
    back = scale * scale * scale * (jnp.sum(products, -1, keepdims=True) * (1.0 / DIN))

    @pl.when(pl.program_id(0) == 0)
    def _():
        g_gain[...] = jnp.zeros_like(g_gain)

    def second(pair, carry):
        at, g, sig, y, gated = parts(pair)
        incoming = grad[:, at]
        g_gain[:, at] += jnp.sum((incoming * gated * scale).reshape(BLOCK // 8, 8, LANES), 0)
        g_gated = scale * incoming * gain[:, at] - gated * back
        grad_y = (g_gated * (g * sig)).astype(bf16)
        g_y[:, at] = grad_y
        g_gate[:, at] = (g_gated * y * (sig * (1.0 + g * (1.0 - sig)))).astype(bf16)
        cols = rows_ref[0, pair].T
        g_read = (jnp.where(low, cols[:, 4:5], cols[:, 5:6]) * grad_y.astype(f32)).astype(bf16)
        g_entering[0, pair] = dot(g_read, rc[...], 0, 0).astype(bf16)
        return carry

    lax.fori_loop(0, PAIRS, second, 0)


def gate_backward(grad, y, gate, gain, wbrc, rows):
    seqs = rows.shape[0]
    wide = pl.BlockSpec((BLOCK, DIN), lambda s: (s, 0))
    return pl.pallas_call(
        gate_back_kernel,
        grid=(seqs,),
        in_specs=[
            wide,
            wide,
            wide,
            pl.BlockSpec((1, DIN), lambda s: (0, 0)),
            pl.BlockSpec((BLOCK, STATE), lambda s: (s, 1)),
            pl.BlockSpec((1, PAIRS, 8, BLOCK), lambda s: (s, 0, 0, 0)),
        ],
        out_specs=[
            wide,
            wide,
            pl.BlockSpec((1, PAIRS, LANES, STATE), lambda s: (s, 0, 0, 0)),
            pl.BlockSpec((8, DIN), lambda s: (0, 0)),
        ],
        out_shape=[
            jax.ShapeDtypeStruct((seqs * BLOCK, DIN), bf16),
            jax.ShapeDtypeStruct((seqs * BLOCK, DIN), bf16),
            jax.ShapeDtypeStruct((seqs, PAIRS, LANES, STATE), bf16),
            jax.ShapeDtypeStruct((8, DIN), f32),
        ],
        compiler_params=params(("arbitrary",)),
        cost_estimate=pl.CostEstimate(
            flops=2 * seqs * BLOCK * DIN * STATE,
            bytes_accessed=seqs * BLOCK * DIN * 12,
            transcendentals=2 * seqs * BLOCK * DIN,
        ),
        name="gate_backward",
    )(grad, y, gate, gain, wbrc, rows)


def scan_back_kernel(
    raw, halo, grad, par, rows_ref, wbrc, entering, g_states,
    g_raw, g_halo, g_par, g_rows,
    ext, gext, g_act, scores, g_scores, g_wb, g_rc,
):
    step = pl.program_id(1)

    @pl.when(step == 0)
    def _():
        scores[...] = dot(wbrc[:, STATE:], wbrc[:, :STATE], 1, 1)
        g_scores[...] = jnp.zeros_like(g_scores)
        g_wb[...] = jnp.zeros_like(g_wb)
        g_rc[...] = jnp.zeros_like(g_rc)

    conv = convolve(ext, raw[...], halo[...], par)
    sig = jax.nn.sigmoid(conv)
    g_par[...] = jnp.zeros_like(g_par)

    @pl.when(step < PAIRS)
    def _():
        x = (conv * sig).astype(bf16).astype(f32)
        gy = grad[...].astype(f32)
        rows = rows_ref[0, 0]
        cols = rows.T
        low = lane_is_low(BLOCK)
        mask = causal_mask()
        wb = wbrc[:, :STATE]
        rc = wbrc[:, STATE:]
        ent = entering[0, 0]
        g_st = g_states[0, 0]

        def head_sums(values):
            first = jnp.sum(jnp.where(low, values, 0.0), -1, keepdims=True)
            second = jnp.sum(jnp.where(low, 0.0, values), -1, keepdims=True)
            return first, second

        e_cum = jnp.where(low, cols[:, 4:5], cols[:, 5:6])
        weight = jnp.where(low, cols[:, 6:7] * cols[:, 0:1], cols[:, 7:8] * cols[:, 1:2])
        readout = dot(rc, ent, 1, 1)
        g_read = e_cum * gy
        read_sums = head_sums(g_read * readout)
        g_rc[...] += dot(g_read.astype(bf16), ent, 1, 0)
        spread_back = dot(wb, g_st, 1, 1)
        weight_sums = head_sums(x * spread_back)
        g_wb[...] += dot((weight * x).astype(bf16), g_st, 1, 0)
        g_x = par[CONV + 1 : CONV + 2, :] * gy + weight * spread_back
        state_products = g_st.astype(f32) * ent.astype(f32)
        last = lax.broadcasted_iota(jnp.int32, (BLOCK, 1), 0) == BLOCK - 1
        lane = lax.broadcasted_iota(jnp.int32, (BLOCK, LANES), 1)
        columns = jnp.zeros((BLOCK, LANES), f32)
        row_parts = []
        for a in range(2):
            mine = low if a == 0 else jnp.logical_not(low)
            x_a = jnp.where(mine, x, 0.0).astype(bf16)
            gy_a = jnp.where(mine, gy, 0.0).astype(bf16)
            dt_row = rows[a : a + 1, :]
            g_mixing = dot(gy_a, x_a, 1, 1)
            spread = cols[:, 2 + a : 3 + a] - rows[2 + a : 3 + a, :]
            decay = jnp.exp(jnp.where(mask, spread, NEG))
            s = scores[...]
            mixing = (s * decay * dt_row).astype(bf16)
            g_x = g_x + dot(mixing, gy_a, 0, 0)
            t = g_mixing * decay
            g_scores[...] += t * dt_row
            q = t * s
            row_sum = jnp.sum(q * dt_row, -1, keepdims=True)
            col_sum = jnp.sum(q, 0, keepdims=True)
            w_col = cols[:, 6 + a : 7 + a] * cols[:, a : a + 1]
            weighted = weight_sums[a] * w_col
            e_total = jnp.exp(rows[2 + a : 3 + a, BLOCK - 1 :])
            pieces = state_products[a * HEAD_DIM : (a + 1) * HEAD_DIM, :]
            g_total = e_total * jnp.sum(jnp.sum(pieces, 0, keepdims=True), 1, keepdims=True)
            g_total = g_total + jnp.sum(weighted, 0, keepdims=True)
            g_cum = row_sum + read_sums[a] - weighted + jnp.where(last, g_total, 0.0)
            g_dt = weight_sums[a] * cols[:, 6 + a : 7 + a]
            columns = jnp.where(lane == a, g_cum, columns)
            columns = jnp.where(lane == 2 + a, g_dt, columns)
            row_parts.append((-dt_row * col_sum, col_sum))
        turned = columns.T[0:8, :]
        row = lax.broadcasted_iota(jnp.int32, (8, BLOCK), 0)
        for a in range(2):
            turned = turned + jnp.where(row == a, row_parts[a][0], 0.0)
            turned = turned + jnp.where(row == 2 + a, row_parts[a][1], 0.0)
        g_rows[0, 0] = turned
        g_act[...] = g_x
        g_par[CONV + 1 : CONV + 2, :] = jnp.sum(gy * x, 0, keepdims=True)

    @pl.when(step == PAIRS)
    def _():
        g_s = g_scores[...]
        g_high = g_s.astype(bf16)
        g_low = (g_s - g_high.astype(f32)).astype(bf16)
        wb = wbrc[:, :STATE]
        rc = wbrc[:, STATE:]
        g_act[...] = g_wb[...] + dot(g_high, rc, 0, 0) + dot(g_low, rc, 0, 0)
        g_rc[...] = g_rc[...] + dot(g_high, wb, 1, 0) + dot(g_low, wb, 1, 0)

    @pl.when(step == PAIRS + 1)
    def _():
        g_act[...] = g_rc[...]

    g_conv = g_act[...] * (sig * (1.0 + conv * (1.0 - sig)))
    gext[0:HALO, :] = jnp.zeros((HALO, LANES), f32)
    gext[HALO : HALO + BLOCK, :] = g_conv
    gext[HALO + BLOCK :, :] = jnp.zeros((HALO, LANES), f32)
    inside = jnp.zeros((BLOCK, LANES), f32)
    before = jnp.zeros((HALO, LANES), f32)
    for tap in range(CONV):
        ahead = CONV - 1 - tap
        factor = par[tap : tap + 1, :]
        inside = inside + factor * gext[pl.ds(HALO + ahead, BLOCK), :]
        before = before + factor * gext[pl.ds(ahead, HALO), :]
        g_par[tap : tap + 1, :] = jnp.sum(
            g_conv * ext[pl.ds(HALO - CONV + 1 + tap, BLOCK), :], 0, keepdims=True
        )
    g_par[CONV : CONV + 1, :] = jnp.sum(g_conv, 0, keepdims=True)
    g_raw[...] = inside.astype(bf16)
    g_halo[...] = before


def scan_backward(proj, grad, par, rows, wbrc, entering, g_states):
    seqs = rows.shape[0]
    halo_at = seqs * BLOCK // HALO

    def clip(p):
        return jnp.minimum(p, PAIRS - 1)

    small = pl.BlockSpec((1, 1, LANES, STATE), lambda s, p: (s, clip(p), 0, 0))
    return pl.pallas_call(
        scan_back_kernel,
        grid=(seqs, PAIRS + 2),
        in_specs=[
            pl.BlockSpec((BLOCK, LANES), lambda s, p: (s, p)),
            pl.BlockSpec((HALO, LANES), lambda s, p: (halo_at + s, p)),
            pl.BlockSpec((BLOCK, LANES), lambda s, p: (s, clip(p))),
            pl.BlockSpec((8, LANES), lambda s, p: (0, p)),
            pl.BlockSpec((1, 1, 8, BLOCK), lambda s, p: (s, clip(p), 0, 0)),
            pl.BlockSpec((BLOCK, 2 * STATE), lambda s, p: (s, 0)),
            small,
            small,
        ],
        out_specs=[
            pl.BlockSpec((BLOCK, LANES), lambda s, p: (s, p)),
            pl.BlockSpec((HALO, LANES), lambda s, p: (s, p)),
            pl.BlockSpec((8, LANES), lambda s, p: (s, p)),
            pl.BlockSpec((1, 1, 8, BLOCK), lambda s, p: (s, clip(p), 0, 0)),
        ],
        out_shape=[
            jax.ShapeDtypeStruct((seqs * BLOCK, REST), bf16),
            jax.ShapeDtypeStruct((seqs * HALO, XBC), f32),
            jax.ShapeDtypeStruct((seqs * 8, XBC), f32),
            jax.ShapeDtypeStruct((seqs, PAIRS, 8, BLOCK), f32),
        ],
        scratch_shapes=[
            pltpu.VMEM((BLOCK + HALO, LANES), f32),
            pltpu.VMEM((BLOCK + 2 * HALO, LANES), f32),
            pltpu.VMEM((BLOCK, LANES), f32),
            pltpu.VMEM((BLOCK, BLOCK), f32),
            pltpu.VMEM((BLOCK, BLOCK), f32),
            pltpu.VMEM((BLOCK, STATE), f32),
            pltpu.VMEM((BLOCK, STATE), f32),
        ],
        compiler_params=params(("arbitrary", "arbitrary")),
        cost_estimate=pl.CostEstimate(
            flops=seqs * PAIRS * 10 * BLOCK * BLOCK * LANES,
            bytes_accessed=seqs * BLOCK * DIN * 6,
            transcendentals=seqs * HEADS * BLOCK * BLOCK,
        ),
        name="scan_backward",
    )(proj, proj, grad, par, rows, wbrc, entering, g_states)


def gather_weight(shard, seq_total, seq_rank):
    piece = shard.shape[0] // seq_total
    mine = lax.dynamic_slice_in_dim(shard, seq_rank * piece, piece, 0)
    return lax.all_gather(mine, ("dp", "seq"), axis=0, tiled=True)


def reduce_weight(grad):
    mine = lax.psum_scatter(grad, ("dp", "seq"), scatter_dimension=0, tiled=True)
    return lax.all_gather(mine, "seq", axis=0, tiled=True)


def shift(values, total, by):
    if by > 0:
        pairs = [(i, i + 1) for i in range(total - 1)]
    else:
        pairs = [(i + 1, i) for i in range(total - 1)]
    return lax.ppermute(values, "seq", pairs)


def exchange(values):
    return lax.all_to_all(values, "seq", split_axis=0, concat_axis=0, tiled=True)


def carry_states(states, decays, seq_total, forward):
    shape = states.shape
    items = shape[0] // seq_total
    blocks = states.reshape((seq_total, items) + shape[1:])
    running = jnp.zeros(blocks.shape[1:], f32)
    found = [None] * seq_total
    for at in range(seq_total) if forward else reversed(range(seq_total)):
        found[at] = running.astype(bf16)
        running = decays[at][:, None, None] * running + blocks[at].astype(f32)
    return jnp.stack(found, 0).reshape(shape)


def local(
    hidden, lengths, cotangent, norm_gain, in_weight, conv_weight, conv_bias,
    dt_bias, decay_log, skip_gain, gate_gain, out_weight,
):
    seq_total = lax.axis_size("seq")
    seq_rank = lax.axis_index("seq")
    data_total = lax.axis_size("dp")
    data_rank = lax.axis_index("dp")
    seqs = hidden.shape[0]
    tokens = seqs * BLOCK
    items = seqs * HEADS // seq_total
    positions = seq_rank * BLOCK + jnp.arange(BLOCK)
    valid = (positions[None, :] < lengths[:, None]).astype(f32).reshape(tokens, 1)

    small = lax.all_gather(
        jnp.concatenate(
            [
                norm_gain,
                conv_weight.reshape(LAYERS, -1),
                conv_bias,
                dt_bias,
                decay_log,
                skip_gain,
                gate_gain,
            ],
            1,
        ),
        "dp",
        axis=0,
    ).astype(f32)
    widths = [D, CONV * XBC, XBC, HEADS, HEADS, HEADS, DIN]
    split_at = []
    running = 0
    for width in widths:
        split_at.append((running, width // data_total))
        running += width // data_total

    def small_of(member, layer):
        start, size = split_at[member]
        values = small[:, layer, start : start + size]
        if member == 1:
            taps = values.reshape(data_total, CONV, XBC // data_total)
            return taps.transpose(1, 0, 2).reshape(CONV, XBC)
        return values.reshape(-1)

    weights = []
    for layer in range(LAYERS):
        weights.append(
            (
                gather_weight(in_weight[layer, :, DIN:], seq_total, seq_rank),
                gather_weight(in_weight[layer, :, :DIN], seq_total, seq_rank),
                gather_weight(out_weight[layer], seq_total, seq_rank),
            )
        )

    lower = (jnp.arange(BLOCK)[:, None] >= jnp.arange(BLOCK)[None, :]).astype(f32)
    h = hidden.astype(f32).reshape(tokens, D)
    kept = []
    squares = []
    for layer in range(LAYERS):
        gain = small_of(0, layer)
        taps, bias = small_of(1, layer), small_of(2, layer)
        step_bias, log_rate = small_of(3, layer), small_of(4, layer)
        skip, gated_gain = small_of(5, layer), small_of(6, layer)[None]
        w_rest, w_gate, w_out = weights[layer]
        par = jnp.concatenate(
            [
                taps,
                bias[None],
                jnp.concatenate([jnp.repeat(skip, HEAD_DIM), jnp.zeros((2 * STATE,), f32)])[None],
                jnp.zeros((2, XBC), f32),
            ],
            0,
        )
        halo = shift(h.reshape(seqs, BLOCK, D)[:, BLOCK - HALO :], seq_total, 1)
        h_more = jnp.concatenate([h, halo.reshape(seqs * HALO, D)], 0)
        scale = lax.rsqrt(jnp.mean(h_more * h_more, -1, keepdims=True) + epsilon)
        normed_more = (h_more * scale * gain).astype(bf16)
        normed = normed_more[:tokens]
        proj = dot(normed_more, w_rest, 1, 0).astype(bf16)
        gate = dot(normed, w_gate, 1, 0).astype(bf16)
        step_in = proj[:tokens, XBC:].reshape(seqs, BLOCK, HEADS).astype(f32).transpose(0, 2, 1)
        step_in = step_in + step_bias[:, None]
        dt = jax.nn.softplus(step_in)
        speed = jnp.exp(log_rate)[:, None]
        cum = jnp.einsum("shj,ij->shi", -dt * speed, lower, precision=highest)
        total = cum[..., -1]
        rows = jnp.stack([dt, cum, jnp.exp(cum), jnp.exp(total[..., None] - cum)], 2)
        rows = rows.reshape(seqs, PAIRS, 2, 4, BLOCK).transpose(0, 1, 3, 2, 4)
        rows = rows.reshape(seqs, PAIRS, 8, BLOCK)
        totals = lax.all_gather(total.reshape(-1), "seq", axis=0)
        decays = jnp.exp(lax.dynamic_slice_in_dim(totals, seq_rank * items, items, 1))
        direct, states, wbrc = scan_forward(proj, par, rows)
        entering = exchange(
            carry_states(
                exchange(states.reshape(seqs * HEADS, HEAD_DIM, STATE)), decays, seq_total, True
            )
        ).reshape(states.shape)
        y, gated = gate_forward(direct, gate, wbrc, rows, entering, gated_gain)
        mixer = dot(gated, w_out, 1, 0)
        squares.append(jnp.sum(h * h * valid))
        squares.append(jnp.sum(mixer * mixer * valid))
        kept.append(
            (h, scale[:tokens], gain, normed, proj, gate, step_in, dt, speed, par, rows, decays,
             wbrc, entering, y, gated, gated_gain)
        )
        h = h + mixer
    output = (h * valid).reshape(hidden.shape)

    g = cotangent.astype(f32).reshape(tokens, D) * valid
    large_in = [None] * LAYERS
    large_out = [None] * LAYERS
    sums = [None] * LAYERS
    for layer in reversed(range(LAYERS)):
        (h_in, scale, gain, normed, proj, gate, step_in, dt, speed, par, rows, decays,
         wbrc, entering, y, gated, gated_gain) = kept[layer]
        w_rest, w_gate, w_out = weights[layer]
        g_low = g.astype(bf16)
        grad_out = reduce_weight(dot(gated, g_low, 0, 0).astype(bf16))
        g_gated = dot(g_low, w_out, 1, 1)
        g_y, g_gate, g_entering, g_gated_gain = gate_backward(
            g_gated, y, gate, gated_gain, wbrc, rows
        )
        grad_gate = reduce_weight(dot(normed, g_gate, 0, 0).astype(bf16))
        g_states = exchange(
            carry_states(
                exchange(g_entering.reshape(seqs * HEADS, HEAD_DIM, STATE)),
                decays,
                seq_total,
                False,
            )
        ).reshape(g_entering.shape)
        g_raw, g_halo, g_par, g_rows = scan_backward(
            proj, g_y, par, rows, wbrc, entering, g_states
        )
        g_rows = g_rows[:, :, :4].reshape(seqs, PAIRS, 2, 2, BLOCK).transpose(2, 0, 1, 3, 4)
        g_rows = g_rows.reshape(2, seqs, HEADS, BLOCK)
        g_rate = jnp.einsum("shi,ij->shj", g_rows[0], lower, precision=highest)
        g_dt = g_rows[1] - speed * g_rate
        g_step = g_dt * jax.nn.sigmoid(step_in)
        g_log = jnp.sum(-dt * speed * g_rate, (0, 2))
        from_next = shift(g_halo.reshape(seqs, HALO, XBC), seq_total, -1)
        tail = g_raw.reshape(seqs, BLOCK, REST)[:, BLOCK - HALO :, :XBC].astype(f32) + from_next
        g_rest = g_raw.reshape(seqs, BLOCK, REST)
        g_rest = lax.dynamic_update_slice(g_rest, tail.astype(bf16), (0, BLOCK - HALO, 0))
        g_rest = lax.dynamic_update_slice(
            g_rest, g_step.transpose(0, 2, 1).astype(bf16), (0, 0, XBC)
        ).reshape(tokens, REST)
        grad_rest = reduce_weight(dot(normed, g_rest, 0, 0).astype(bf16))
        g_normed = dot(g_gate, w_gate, 1, 1) + dot(g_rest, w_rest, 1, 1)
        scaled = g_normed * gain
        inner = jnp.mean(scaled * h_in, -1, keepdims=True)
        g = g + scale * scaled - h_in * (scale * scale * scale * inner)
        g_gain = jnp.sum(g_normed * h_in * scale, 0)
        g_par = jnp.sum(g_par.reshape(seqs, 8, XBC), 0)
        sums[layer] = (
            g_gain,
            g_par[:CONV].reshape(-1),
            g_par[CONV],
            jnp.sum(g_step, (0, 2)),
            g_log,
            jnp.sum(g_par[CONV + 1, :DIN].reshape(HEADS, HEAD_DIM), 1),
            jnp.sum(g_gated_gain, 0),
        )
        large_in[layer] = jnp.concatenate([grad_gate, grad_rest], 1).astype(f32)
        large_out[layer] = grad_out.astype(f32)

    flat = jnp.concatenate(
        [part for layer_sums in sums for part in layer_sums]
        + [jnp.stack(squares), jnp.sum(valid)[None]]
    )
    flat = lax.psum(flat, ("dp", "seq"))
    norm_stats = jnp.sqrt(flat[-5:-1].reshape(LAYERS, 2) / (flat[-1] * D))
    whole = flat[:-5].reshape(LAYERS, -1)
    found = []
    start = 0
    for member, width in enumerate(widths):
        values = whole[:, start : start + width]
        start += width
        piece = width // data_total
        if member == 1:
            values = values.reshape(LAYERS, CONV, XBC)
            piece = XBC // data_total
        found.append(
            lax.dynamic_slice_in_dim(values, data_rank * piece, piece, values.ndim - 1)
        )
    return (
        output,
        g.reshape(hidden.shape),
        found[0],
        jnp.stack(large_in, 0),
        found[1],
        found[2],
        found[3],
        found[4],
        found[5],
        found[6],
        jnp.stack(large_out, 0),
        norm_stats,
    )


def solution(mesh):
    return jax.shard_map(
        local,
        mesh=mesh,
        in_specs=(
            P("dp", "seq", None),
            P("dp"),
            P("dp", "seq", None),
            P(None, "dp"),
            P(None, "dp", None),
            P(None, None, "dp"),
            P(None, "dp"),
            P(None, "dp"),
            P(None, "dp"),
            P(None, "dp"),
            P(None, "dp"),
            P(None, "dp", None),
        ),
        out_specs=(
            P("dp", "seq", None),
            P("dp", "seq", None),
            P(None, "dp"),
            P(None, "dp", None),
            P(None, None, "dp"),
            P(None, "dp"),
            P(None, "dp"),
            P(None, "dp"),
            P(None, "dp"),
            P(None, "dp"),
            P(None, "dp", None),
            P(),
        ),
        check_vma=False,
    )
```
